256 devices in a mesh: fsdp: 32 (over z, y_lo, core), tp: 8 (over x, y_hi).
Axes of the slice: x: 4, y: 4 (y_hi: 2, y_lo: 2; y = y_hi * 2 + y_lo), z: 8, core: 2. Of those that a mesh axis runs over, the one named last changes fastest.
Arguments:
- tokens: bfloat16 [2048, 8192], P('tp', 'fsdp'), may hold values from -6 to 6
- gate_blocks: bfloat16 [256, 22, 128, 128], P(('fsdp', 'tp')), may hold values from -0.109375 to 0.109375
- up_blocks: bfloat16 [256, 22, 128, 128], P(('fsdp', 'tp')), may hold values from -0.109375 to 0.109375
- down_blocks: bfloat16 [256, 22, 128, 128], P(('fsdp', 'tp')), may hold values from -0.0546875 to 0.0546875
- gate_index: int32 [256, 22], P('fsdp'), may hold values from 0 to 63, as said below
- up_index: int32 [256, 22], P('fsdp'), may hold values from 0 to 63, as said below
- down_index: int32 [256, 22], P('fsdp'), may hold values from 0 to 63, as said below
- gate_count: int32 [256], P('fsdp'), may hold values from 14 to 22
- up_count: int32 [256], P('fsdp'), may hold values from 14 to 22
- down_count: int32 [256], P('fsdp'), may hold values from 14 to 22
Outputs:
- mixed: bfloat16 [2048, 8192], P('tp', 'fsdp')
The draws below stay inside these ranges and needn't reach their ends.
Inputs may be any that keep to these rules, and one draw needn't show every extreme that they name: `gate_index`: in each row the first gate_count entries name the kept row blocks of that block column; the 22 entries of a row are different numbers. `up_index`: in each row the first up_count entries name the kept row blocks of that block column; the 22 entries of a row are different numbers. `down_index`: in each row the first down_count entries name the kept column blocks of that block row; the 22 entries of a row are different numbers.
All inputs are finite; a program needn't handle non-finite values.
Results may differ from the reference program's by a relative error of at most 0.0049.
Values may be sent and summed in bfloat16 or wider, within the bound.
No kernel may reach another device: no remote copies, remote signals or barrier semaphores. Data moves between devices by JAX's collectives and lax.ppermute only.
A program may use at most 192 MiB of HBM per device.

```python
import jax
import jax.numpy as jnp
from jax import lax

D = 8192
F = 32768
BLK = 128
KMAX = 22
KMIN = 14
TOKENS = 2048
DB = 64
FB = 256


def draw_index_rows(key):
    row_keys = jax.random.split(key, FB)
    orders = jax.vmap(lambda one_key: jax.random.permutation(one_key, DB))(row_keys)
    return orders[:, :KMAX].astype(jnp.int32)


def draw_count_rows(key):
    first_key, second_key, third_key = jax.random.split(key, 3)
    counts = jax.random.randint(first_key, (FB,), KMIN, KMAX + 1).astype(jnp.int32)
    top_pos = jax.random.randint(second_key, (), 0, FB)
    low_pos = (top_pos + 1 + jax.random.randint(third_key, (), 0, FB - 1)) % FB
    counts = counts.at[top_pos].set(KMAX)
    counts = counts.at[low_pos].set(KMIN)
    return counts


def draw_gate_index(key, part):
    return draw_index_rows(jax.random.fold_in(key, 101))


def draw_up_index(key, part):
    return draw_index_rows(jax.random.fold_in(key, 202))


def draw_down_index(key, part):
    return draw_index_rows(jax.random.fold_in(key, 303))


def draw_gate_count(key, part):
    return draw_count_rows(jax.random.fold_in(key, 404))


def draw_up_count(key, part):
    return draw_count_rows(jax.random.fold_in(key, 505))


def draw_down_count(key, part):
    return draw_count_rows(jax.random.fold_in(key, 606))


def block_levels(stream_key, dims, pieces, least, high):
    factor_of, own = 1.0, jax.random.fold_in(stream_key, 6)
    for dim, parts in pieces:
        draws = jnp.exp(jax.random.uniform(jax.random.fold_in(own, dim), (parts,), jnp.float32, least / len(pieces), high / len(pieces)))
        factor_of = factor_of * jnp.repeat(draws, dims[dim] // parts).reshape([-1 if axis == dim else 1 for axis in range(len(dims))])
    return factor_of


def centred(key, shape, deviation, bound, pieces=(), held_as=jnp.bfloat16):
    level = block_levels(key, shape, pieces, -0.22, 0.18) if pieces else 1.0
    array = jax.random.normal(key, shape, jnp.float32) * deviation * level
    return jnp.minimum(jnp.maximum(array, -bound), bound).astype(held_as)


def setup_inputs(seed: int = 0) -> dict:
    seeds = jax.random.split(jax.random.key(seed), 11)
    return {
        "tokens": centred(seeds[0], (TOKENS, D), 1.0, 6.0, ((0, 8), (1, 32))),
        "gate_blocks": centred(seeds[1], (FB, KMAX, BLK, BLK), (KMAX * BLK) ** -0.5, 0.109375, ((0, 256),)),
        "up_blocks": centred(seeds[2], (FB, KMAX, BLK, BLK), (KMAX * BLK) ** -0.5, 0.109375, ((0, 256),)),
        "down_blocks": centred(seeds[3], (FB, KMAX, BLK, BLK), (F * KMAX // DB) ** -0.5, 0.0546875, ((0, 256),)),
        "gate_index": draw_gate_index(jax.random.fold_in(seeds[10], 71), 0),
        "up_index": draw_up_index(jax.random.fold_in(seeds[10], 71), 0),
        "down_index": draw_down_index(jax.random.fold_in(seeds[10], 71), 0),
        "gate_count": draw_gate_count(jax.random.fold_in(seeds[10], 71), 0),
        "up_count": draw_up_count(jax.random.fold_in(seeds[10], 71), 0),
        "down_count": draw_down_count(jax.random.fold_in(seeds[10], 71), 0),
    }


def project_in(tile_grid, block_set, row_ids, kept_num):
    token_rows = tile_grid.shape[0]
    slot_num = row_ids.shape[1]
    side_len = tile_grid.shape[2]

    def column_block(packed):
        blocks_one, ids_one, count_one = packed
        live_mask = (jnp.arange(slot_num) < count_one).astype(blocks_one.dtype)
        selected = tile_grid[:, ids_one, :].reshape(token_rows, slot_num * side_len)
        panel_mat = (blocks_one * live_mask[:, None, None]).reshape(slot_num * side_len, side_len)
        return jnp.dot(selected, panel_mat, preferred_element_type=jnp.float32)

    column_out = lax.map(column_block, (block_set, row_ids, kept_num))
    return jnp.transpose(column_out, (1, 0, 2)).reshape(token_rows, -1)


def project_out(hidden, block_set, col_ids, kept_num, row_blocks):
    token_rows = hidden.shape[0]
    slot_num = col_ids.shape[1]
    side_len = block_set.shape[2]
    hid_tiles = jnp.transpose(hidden.reshape(token_rows, -1, side_len), (1, 0, 2))

    def advance(running, packed):
        blocks_one, ids_one, count_one, hid_tile = packed
        live_mask = (jnp.arange(slot_num) < count_one).astype(blocks_one.dtype)
        panel_mat = jnp.transpose(blocks_one * live_mask[:, None, None], (1, 0, 2)).reshape(side_len, slot_num * side_len)
        product = jnp.dot(hid_tile, panel_mat, preferred_element_type=jnp.float32).reshape(token_rows, slot_num, side_len)
        return running.at[:, ids_one, :].add(product), None

    start_sum = jnp.zeros((token_rows, row_blocks, side_len), jnp.float32)
    running, _ = lax.scan(advance, start_sum, (block_set, col_ids, kept_num, hid_tiles))
    return running.reshape(token_rows, row_blocks * side_len)


def reference(tokens, gate_blocks, up_blocks, down_blocks, gate_index, up_index, down_index, gate_count, up_count, down_count):
    token_rows = tokens.shape[0]
    side_len = gate_blocks.shape[2]
    row_blocks = tokens.shape[1] // side_len
    tile_grid = tokens.reshape(token_rows, row_blocks, side_len)
    gate = project_in(tile_grid, gate_blocks, gate_index, gate_count)
    up_val = project_in(tile_grid, up_blocks, up_index, up_count)
    hidden = (jax.nn.silu(gate) * up_val).astype(jnp.bfloat16)
    mixed = project_out(hidden, down_blocks, down_index, down_count, row_blocks)
    return mixed.astype(jnp.bfloat16)
```

```python
import functools

import jax
import jax.numpy as jnp
from jax import lax
from jax.experimental import pallas as pl
from jax.experimental.pallas import tpu as pltpu
from jax.sharding import Mesh
from jax.sharding import PartitionSpec as P


BF16 = jnp.bfloat16
F32 = jnp.float32
NZ, NY, NX = 8, 4, 4
BLK = 128
SLOTS = 22
FBS = 64
HALF = 128
ROWS = 2 * HALF
PER = 4
AXES = ("z", "ylo", "core", "x", "yhi")


def y_pos(y):
    y = y % NY
    return (y % 2) * 2 + y // 2


def shift_z(v, d):
    return lax.ppermute(v, "z", [(i, (i + d) % NZ) for i in range(NZ)])


def shift_x(v, d):
    return lax.ppermute(v, "x", [(i, (i + d) % NX) for i in range(NX)])


def shift_y(v, d):
    return lax.ppermute(v, ("ylo", "yhi"), [(y_pos(i), y_pos(i + d)) for i in range(NY)])


def swap_core(v):
    return lax.ppermute(v, "core", [(0, 1), (1, 0)])


def column_step(tab, x_ref, w_ref, acc_ref, slot, tab_own, row):
    def project(which):
        total = None
        for pair in range(SLOTS // 2):
            base = tab_own + (which * 8) * SLOTS + row * SLOTS + 2 * pair
            lhs = jnp.concatenate([x_ref[tab[base]], x_ref[tab[base + 1]]], axis=1)
            first = which * SLOTS + 2 * pair
            rhs = w_ref[slot, first : first + 2].reshape(2 * BLK, BLK)
            part = jnp.dot(lhs, rhs, preferred_element_type=F32)
            total = part if total is None else total + part
        return total

    gate = project(0)
    up = project(1)
    hidden = (gate / (1.0 + jnp.exp(-gate)) * up).astype(BF16)
    for pair in range(SLOTS // 2):
        base = tab_own + 2 * 8 * SLOTS + row * SLOTS + 2 * pair
        first = 2 * SLOTS + 2 * pair
        rhs = jnp.concatenate([w_ref[slot, first], w_ref[slot, first + 1]], axis=1)
        part = jnp.dot(hidden, rhs, preferred_element_type=F32)
        one, two = tab[base], tab[base + 1]
        acc_ref[one] += part[:, :BLK]
        acc_ref[two] += part[:, BLK:]


def token_copies(meta, pieces, x_ref, sem):
    z, y = meta[0], meta[1]
    copies = []
    for dz, lo, hi, ref in pieces:
        zz = lax.rem(z + dz, NZ)
        for dy in range(lo, hi):
            yy = lax.rem(y + dy, NY)
            fb = zz * 8 + lax.rem(yy, 2) * PER
            at = pl.multiple_of((yy // 2) * HALF, HALF)
            copies.append(
                pltpu.make_async_copy(
                    ref.at[dy - lo],
                    x_ref.at[pl.ds(fb, PER), pl.ds(at, HALF), :],
                    sem.at[dz * NY + dy],
                )
            )
    return copies


def first_kernel(tab, meta, *refs):
    toks = refs[:9]
    weights = refs[9:15]
    acc_ref, x_out, x_ref, w_ref, tsem, wsem, osem = refs[15:]
    y0, p1, p2, p3, m1, m2, m3, h0, h1 = toks
    pieces = [
        (0, 0, 4, y0), (7, 0, 4, p1), (6, 0, 4, p2), (5, 0, 4, p3), (1, 0, 4, m1),
        (2, 0, 4, m2), (3, 0, 4, m3), (4, 0, 2, h0), (4, 2, 4, h1),
    ]
    copies = token_copies(meta, pieces, x_ref, tsem)
    for copy in copies:
        copy.start()
    wcopies = [
        pltpu.make_async_copy(ref, w_ref.at[i], wsem.at[i]) for i, ref in enumerate(weights)
    ]
    for copy in wcopies:
        copy.start()
    x_ref[FBS] = jnp.zeros((ROWS, BLK), BF16)
    acc_ref[...] = jnp.zeros_like(acc_ref)
    for copy in copies:
        copy.wait()
    out = pltpu.make_async_copy(x_ref.at[pl.ds(0, FBS)], x_out, osem)
    out.start()
    for copy in wcopies:
        copy.wait()

    @pl.loop(0, 6)
    def _(i):
        chip = i // 2
        row = meta[2 + chip]
        tab_own = lax.rem(i, 2) * (3 * 8 * SLOTS)
        column_step(tab, x_ref, w_ref, acc_ref, i, tab_own, row)

    out.wait()


A_OUT = ((8,), (8,), (8,), (4,), (4,))


def last_kernel(tab, meta, acc_in, x_in, wa, wb, wpa, wpb, *refs):
    outs = refs[:14]
    acc_ref, x_ref, w_ref, sem = refs[14:]
    cut = wa.shape[0]
    copies = [
        pltpu.make_async_copy(x_in, x_ref.at[pl.ds(0, FBS)], sem.at[0]),
        pltpu.make_async_copy(wa, w_ref.at[0, pl.ds(0, cut)], sem.at[1]),
        pltpu.make_async_copy(wb, w_ref.at[0, pl.ds(cut, cut)], sem.at[2]),
        pltpu.make_async_copy(wpa, w_ref.at[1, pl.ds(0, cut)], sem.at[3]),
        pltpu.make_async_copy(wpb, w_ref.at[1, pl.ds(cut, cut)], sem.at[4]),
        pltpu.make_async_copy(acc_in, acc_ref, sem.at[5]),
    ]
    for copy in copies:
        copy.start()
    x_ref[FBS] = jnp.zeros((ROWS, BLK), BF16)
    for copy in copies:
        copy.wait()

    @pl.loop(0, 2)
    def _(i):
        column_step(tab, x_ref, w_ref, acc_ref, i, i * (3 * 8 * SLOTS), meta[5])

    z, y = meta[0], meta[1]

    def chunk(dz, dy, color):
        zz = lax.rem(z + dz, NZ)
        yy = lax.rem(y + dy, NY)
        fb = zz * 8 + lax.rem(yy, 2) * PER + 2 * color
        at = pl.multiple_of((yy // 2) * HALF, HALF)
        return acc_ref[pl.ds(fb, 2), pl.ds(at, HALF), :].astype(BF16)

    a0, yp1, ym1, a1a, a3b, b0, zp1, zp2, zp3, zp4, zm1, zm2, zm3, zm4 = outs
    for d in range(4):
        lo, hi = d, d + 4
        a0[lo] = chunk(lo, 0, 0)
        a0[hi] = chunk(hi, 0, 0)
        yp1[d] = chunk(lo, 2, 0)
        yp1[d + 4] = chunk(hi, 1, 0)
        ym1[d] = chunk(hi, 2, 0)
        ym1[d + 4] = chunk(lo, 3, 0)
        a1a[d] = chunk(lo, 1, 0)
        a3b[d] = chunk(hi, 3, 0)
        b0[d] = chunk(0, d, 1)
    for step, (zp, zm) in enumerate(((zp1, zm1), (zp2, zm2), (zp3, zm3)), 1):
        for d in range(2):
            zp[d] = chunk(5 - step, d, 1)
            zp[d + 2] = chunk(4 - step, d + 2, 1)
            zm[d] = chunk(3 + step, d + 2, 1)
            zm[d + 2] = chunk(4 + step, d, 1)
    for d in range(2):
        zp4[d] = chunk(1, d, 1)
        zm4[d] = chunk(7, d + 2, 1)


OUT_LEAD = (8, 8, 8, 4, 4, 4, 4, 4, 4, 2, 4, 4, 4, 2)


def run_first(tab, meta, toks, weights):
    anyspec = pl.BlockSpec(memory_space=pl.ANY)
    smem = pl.BlockSpec(memory_space=pltpu.SMEM)
    return pl.pallas_call(
        first_kernel,
        out_shape=(
            jax.ShapeDtypeStruct((FBS + 1, ROWS, BLK), F32),
            jax.ShapeDtypeStruct((FBS, ROWS, BLK), BF16),
        ),
        in_specs=[smem, smem] + [anyspec] * 15,
        out_specs=(pl.BlockSpec(memory_space=pltpu.VMEM), anyspec),
        scratch_shapes=[
            pltpu.VMEM((FBS + 1, ROWS, BLK), BF16),
            pltpu.VMEM((6, 3 * SLOTS, BLK, BLK), BF16),
            pltpu.SemaphoreType.DMA((NZ * NY,)),
            pltpu.SemaphoreType.DMA((6,)),
            pltpu.SemaphoreType.DMA,
        ],
        cost_estimate=pl.CostEstimate(
            flops=2 * 6 * 3 * SLOTS * ROWS * BLK * BLK, bytes_accessed=30 << 20, transcendentals=0
        ),
        name="first",
    )(tab, meta, *toks, *weights)


def run_last(tab, meta, acc, x_all, halves):
    anyspec = pl.BlockSpec(memory_space=pl.ANY)
    smem = pl.BlockSpec(memory_space=pltpu.SMEM)
    return pl.pallas_call(
        last_kernel,
        out_shape=tuple(jax.ShapeDtypeStruct((n, 2, HALF, BLK), BF16) for n in OUT_LEAD),
        in_specs=[smem, smem] + [anyspec] * 6,
        out_specs=tuple(pl.BlockSpec(memory_space=pltpu.VMEM) for _ in OUT_LEAD),
        scratch_shapes=[
            pltpu.VMEM((FBS + 1, ROWS, BLK), F32),
            pltpu.VMEM((FBS + 1, ROWS, BLK), BF16),
            pltpu.VMEM((2, 3 * SLOTS, BLK, BLK), BF16),
            pltpu.SemaphoreType.DMA((6,)),
        ],
        cost_estimate=pl.CostEstimate(
            flops=2 * 2 * 3 * SLOTS * ROWS * BLK * BLK, bytes_accessed=20 << 20, transcendentals=0
        ),
        name="last",
    )(tab, meta, acc, x_all, *halves)


def add(*terms):
    total = terms[0].astype(F32)
    for term in terms[1:]:
        total = total + term.astype(F32)
    return total


def reduce_scatter(parts):
    a0, yp1, ym1, a1a, a3b, b0, zp1, zp2, zp3, zp4, zm1, zm2, zm3, zm4 = parts
    rp = shift_z(zp1, 1)
    rm = shift_z(zm1, -1)
    ryp = shift_y(yp1, 1)
    rym = shift_y(ym1, -1)
    rp = shift_z(add(zp2, rp).astype(BF16), 1)
    rm = shift_z(add(zm2, rm).astype(BF16), -1)
    ryp2 = shift_y(add(a1a, ryp[:4]).astype(BF16), 1)
    rym2 = shift_y(add(a3b, rym[:4]).astype(BF16), -1)
    rp = shift_z(add(zp3, rp).astype(BF16), 1)
    rm = shift_z(add(zm3, rm).astype(BF16), -1)
    rp4 = shift_z(add(zp4, rp[:2]).astype(BF16), 1)
    rm4 = shift_z(add(zm4, rm[:2]).astype(BF16), -1)
    ay = [add(a0[d], ryp2[d], rym[4 + d]) for d in range(4)] + [
        add(a0[4 + d], ryp[4 + d], rym2[d]) for d in range(4)
    ]
    a_sum = ay[0]
    a_in = [shift_z(ay[d].astype(BF16), d) for d in range(1, NZ)]
    bz = [add(b0[d], rp4[d], rm[2 + d]) for d in range(2)] + [
        add(b0[2 + d], rp[2 + d], rm4[d]) for d in range(2)
    ]
    b_in = [shift_y(bz[d].astype(BF16), d) for d in range(1, NY)]
    return add(a_sum, *a_in).astype(BF16), add(bz[0], *b_in).astype(BF16)


def body(
    tokens, gate_blocks, up_blocks, down_blocks,
    gate_index, up_index, down_index, gate_count, up_count, down_count,
):
    core = lax.axis_index("core")
    x, yhi = lax.axis_index("x"), lax.axis_index("yhi")
    z = lax.axis_index("z")
    y = 2 * yhi + lax.axis_index("ylo")

    own = jnp.concatenate([gate_blocks[0], up_blocks[0], down_blocks[0]], axis=0)
    left = shift_x(own, 1)
    right = shift_x(own, -1)
    cut = 3 * SLOTS // 2
    far_a = shift_x(left[:cut], 1)
    far_b = shift_x(right[cut:], -1)

    def table(index, count):
        live = jnp.arange(SLOTS, dtype=jnp.int32)[None, :] < count[:, None]
        return jnp.where(live, index, FBS)

    tab = jnp.stack(
        [table(gate_index, gate_count), table(up_index, up_count), table(down_index, down_count)]
    )
    tab = jnp.stack([tab, swap_core(tab)]).reshape(-1)
    rows = [lax.rem(x + off, NX) * 2 + yhi for off in (0, 3, 1, 2)]
    meta = jnp.stack([z, y, *rows]).astype(jnp.int32)

    def block_rows(c):
        part = lax.dynamic_slice_in_dim(tokens, c * HALF, HALF, axis=0)
        return jnp.transpose(part.reshape(HALF, 2, BLK), (1, 0, 2))

    keep = block_rows(core)
    got = swap_core(block_rows(1 - core))
    chip = jnp.where(
        core == 0,
        jnp.concatenate([keep, got], axis=0),
        jnp.concatenate([got, keep], axis=0),
    )
    y0 = jnp.stack([chip, shift_y(chip, -1), shift_y(chip, 2), shift_y(chip, 1)])
    p1, m1 = shift_z(y0, 1), shift_z(y0, -1)
    p2, m2 = shift_z(p1, 1), shift_z(m1, -1)
    p3, m3 = shift_z(p2, 1), shift_z(m2, -1)
    h0, h1 = shift_z(p3[:2], 1), shift_z(m3[2:], -1)

    weights = (own, swap_core(own), left, swap_core(left), right, swap_core(right))
    acc, x_all = run_first(tab, meta, (y0, p1, p2, p3, m1, m2, m3, h0, h1), weights)
    halves = (far_a, far_b, swap_core(far_a), swap_core(far_b))
    parts = run_last(tab, meta, acc, x_all, halves)

    a_fin, b_fin = reduce_scatter(parts)
    mine = jnp.where(core == 0, a_fin, b_fin)
    other = swap_core(jnp.where(core == 0, b_fin, a_fin))
    low = jnp.where(core == 0, mine, other)
    high = jnp.where(core == 0, other, mine)
    out = jnp.stack([low, high])
    return jnp.transpose(out, (0, 2, 1, 3)).reshape(2 * HALF, 2 * BLK)


def solution(mesh):
    fine = Mesh(mesh.devices.reshape(NZ, 2, 2, NX, 2), AXES)
    fsdp, tp = ("z", "ylo", "core"), ("x", "yhi")
    blocks = P(fsdp + tp, None, None, None)
    in_specs = (
        P(tp, fsdp), blocks, blocks, blocks,
        P(fsdp, None), P(fsdp, None), P(fsdp, None), P(fsdp), P(fsdp), P(fsdp),
    )
    return jax.shard_map(
        body, mesh=fine, in_specs=in_specs, out_specs=P(tp, fsdp), check_vma=False
    )
```

```python
import functools

import jax
import jax.numpy as jnp
from jax import lax
from jax.experimental import pallas as pl
from jax.experimental.pallas import tpu as pltpu
from jax.sharding import Mesh
from jax.sharding import PartitionSpec as P


BF16 = jnp.bfloat16
F32 = jnp.float32
NZ, NY, NX = 8, 4, 4
BLK = 128
SLOTS = 22
FBS = 64
HALF = 128
ROWS = 2 * HALF
PER = 4
AXES = ("z", "ylo", "core", "x", "yhi")


def y_pos(y):
    y = y % NY
    return (y % 2) * 2 + y // 2


def shift_z(v, d):
    return lax.ppermute(v, "z", [(i, (i + d) % NZ) for i in range(NZ)])


def shift_x(v, d):
    return lax.ppermute(v, "x", [(i, (i + d) % NX) for i in range(NX)])


def shift_y(v, d):
    return lax.ppermute(v, ("ylo", "yhi"), [(y_pos(i), y_pos(i + d)) for i in range(NY)])


def swap_core(v):
    return lax.ppermute(v, "core", [(0, 1), (1, 0)])


def column_step(tab, x_ref, w_ref, acc_ref, slot, tab_own, row):
    def project(which):
        total = None
        for pair in range(SLOTS // 2):
            base = tab_own + (which * 8) * SLOTS + row * SLOTS + 2 * pair
            lhs = jnp.concatenate([x_ref[tab[base]], x_ref[tab[base + 1]]], axis=1)
            first = which * SLOTS + 2 * pair
            rhs = w_ref[slot, first : first + 2].reshape(2 * BLK, BLK)
            part = jnp.dot(lhs, rhs, preferred_element_type=F32)
            total = part if total is None else total + part
        return total

    gate = project(0)
    up = project(1)
    hidden = (gate / (1.0 + jnp.exp(-gate)) * up).astype(BF16)
    for pair in range(SLOTS // 2):
        base = tab_own + 2 * 8 * SLOTS + row * SLOTS + 2 * pair
        first = 2 * SLOTS + 2 * pair
        rhs = jnp.concatenate([w_ref[slot, first], w_ref[slot, first + 1]], axis=1)
        part = jnp.dot(hidden, rhs, preferred_element_type=F32)
        one, two = tab[base], tab[base + 1]
        acc_ref[one] += part[:, :BLK]
        acc_ref[two] += part[:, BLK:]


def token_copies(meta, pieces, x_ref, sem):
    z, y = meta[0], meta[1]
    copies = []
    for dz, lo, hi, ref in pieces:
        zz = lax.rem(z + dz, NZ)
        for dy in range(lo, hi):
            yy = lax.rem(y + dy, NY)
            fb = zz * 8 + lax.rem(yy, 2) * PER
            at = pl.multiple_of((yy // 2) * HALF, HALF)
            copies.append(
                pltpu.make_async_copy(
                    ref.at[dy - lo],
                    x_ref.at[pl.ds(fb, PER), pl.ds(at, HALF), :],
                    sem.at[dz * NY + dy],
                )
            )
    return copies


def first_kernel(tab, meta, *refs):
    toks = refs[:9]
    weights = refs[9:15]
    acc_ref, x_ref, w_ref, tsem, wsem = refs[15:]
    y0, p1, p2, p3, m1, m2, m3, h0, h1 = toks
    pieces = [
        (0, 0, 4, y0), (7, 0, 4, p1), (6, 0, 4, p2), (5, 0, 4, p3), (1, 0, 4, m1),
        (2, 0, 4, m2), (3, 0, 4, m3), (4, 0, 2, h0), (4, 2, 4, h1),
    ]
    copies = token_copies(meta, pieces, x_ref, tsem)
    for copy in copies:
        copy.start()
    wcopies = [
        pltpu.make_async_copy(ref, w_ref.at[i], wsem.at[i]) for i, ref in enumerate(weights)
    ]
    for copy in wcopies:
        copy.start()
    x_ref[FBS] = jnp.zeros((ROWS, BLK), BF16)
    acc_ref[...] = jnp.zeros_like(acc_ref)
    for copy in copies:
        copy.wait()

    @pl.loop(0, 6)
    def _(i):
        for j, copy in enumerate(wcopies):
            pl.when(i == j)(copy.wait)
        chip = i // 2
        row = meta[2 + chip]
        tab_own = lax.rem(i, 2) * (3 * 8 * SLOTS)
        column_step(tab, x_ref, w_ref, acc_ref, i, tab_own, row)


def last_kernel(tab, meta, acc_in, x_ref, wa, wb, wpa, wpb, *refs):
    del acc_in
    outs = refs[:14]
    acc_ref, w_ref, sem = refs[14:]
    cut = wa.shape[0]
    copies = [
        pltpu.make_async_copy(wa, w_ref.at[0, pl.ds(0, cut)], sem.at[0]),
        pltpu.make_async_copy(wb, w_ref.at[0, pl.ds(cut, cut)], sem.at[1]),
        pltpu.make_async_copy(wpa, w_ref.at[1, pl.ds(0, cut)], sem.at[2]),
        pltpu.make_async_copy(wpb, w_ref.at[1, pl.ds(cut, cut)], sem.at[3]),
    ]
    for copy in copies:
        copy.start()

    @pl.loop(0, 2)
    def _(i):
        for j, copy in enumerate(copies):
            pl.when(i == j // 2)(copy.wait)
        column_step(tab, x_ref, w_ref, acc_ref, i, i * (3 * 8 * SLOTS), meta[5])

    z, y = meta[0], meta[1]

    def chunk(dz, dy, color):
        zz = lax.rem(z + dz, NZ)
        yy = lax.rem(y + dy, NY)
        fb = zz * 8 + lax.rem(yy, 2) * PER + 2 * color
        at = pl.multiple_of((yy // 2) * HALF, HALF)
        return acc_ref[pl.ds(fb, 2), pl.ds(at, HALF), :].astype(BF16)

    a0, yp1, ym1, a1a, a3b, b0, zp1, zp2, zp3, zp4, zm1, zm2, zm3, zm4 = outs
    for d in range(4):
        lo, hi = d, d + 4
        a0[lo] = chunk(lo, 0, 0)
        a0[hi] = chunk(hi, 0, 0)
        yp1[d] = chunk(lo, 2, 0)
        yp1[d + 4] = chunk(hi, 1, 0)
        ym1[d] = chunk(hi, 2, 0)
        ym1[d + 4] = chunk(lo, 3, 0)
        a1a[d] = chunk(lo, 1, 0)
        a3b[d] = chunk(hi, 3, 0)
        b0[d] = chunk(0, d, 1)
    for step, (zp, zm) in enumerate(((zp1, zm1), (zp2, zm2), (zp3, zm3)), 1):
        for d in range(2):
            zp[d] = chunk(5 - step, d, 1)
            zp[d + 2] = chunk(4 - step, d + 2, 1)
            zm[d] = chunk(3 + step, d + 2, 1)
            zm[d + 2] = chunk(4 + step, d, 1)
    for d in range(2):
        zp4[d] = chunk(1, d, 1)
        zm4[d] = chunk(7, d + 2, 1)


OUT_LEAD = (8, 8, 8, 4, 4, 4, 4, 4, 4, 2, 4, 4, 4, 2)


def run_first(tab, meta, toks, weights):
    anyspec = pl.BlockSpec(memory_space=pl.ANY)
    smem = pl.BlockSpec(memory_space=pltpu.SMEM)
    vmem = pl.BlockSpec(memory_space=pltpu.VMEM)
    return pl.pallas_call(
        first_kernel,
        out_shape=(
            jax.ShapeDtypeStruct((FBS + 1, ROWS, BLK), F32),
            jax.ShapeDtypeStruct((FBS + 1, ROWS, BLK), BF16),
        ),
        in_specs=[smem, smem] + [anyspec] * 15,
        out_specs=(vmem, vmem),
        scratch_shapes=[
            pltpu.VMEM((6, 3 * SLOTS, BLK, BLK), BF16),
            pltpu.SemaphoreType.DMA((NZ * NY,)),
            pltpu.SemaphoreType.DMA((6,)),
        ],
        compiler_params=pltpu.CompilerParams(vmem_limit_bytes=20 << 20),
        cost_estimate=pl.CostEstimate(
            flops=2 * 6 * 3 * SLOTS * ROWS * BLK * BLK, bytes_accessed=30 << 20, transcendentals=0
        ),
        name="first",
    )(tab, meta, *toks, *weights)


def run_last(tab, meta, acc, x_all, halves):
    anyspec = pl.BlockSpec(memory_space=pl.ANY)
    smem = pl.BlockSpec(memory_space=pltpu.SMEM)
    vmem = pl.BlockSpec(memory_space=pltpu.VMEM)
    outs = pl.pallas_call(
        last_kernel,
        out_shape=tuple(jax.ShapeDtypeStruct((n, 2, HALF, BLK), BF16) for n in OUT_LEAD)
        + (jax.ShapeDtypeStruct(acc.shape, F32),),
        in_specs=[smem, smem, vmem, vmem] + [anyspec] * 4,
        out_specs=tuple(vmem for _ in OUT_LEAD) + (vmem,),
        input_output_aliases={2: len(OUT_LEAD)},
        scratch_shapes=[
            pltpu.VMEM((2, 3 * SLOTS, BLK, BLK), BF16),
            pltpu.SemaphoreType.DMA((4,)),
        ],
        compiler_params=pltpu.CompilerParams(vmem_limit_bytes=16 << 20),
        cost_estimate=pl.CostEstimate(
            flops=2 * 2 * 3 * SLOTS * ROWS * BLK * BLK, bytes_accessed=20 << 20, transcendentals=0
        ),
        name="last",
    )(tab, meta, acc, x_all, *halves)
    return outs[: len(OUT_LEAD)]


def add(*terms):
    total = terms[0].astype(F32)
    for term in terms[1:]:
        total = total + term.astype(F32)
    return total


def reduce_scatter(parts):
    a0, yp1, ym1, a1a, a3b, b0, zp1, zp2, zp3, zp4, zm1, zm2, zm3, zm4 = parts
    rp = shift_z(zp1, 1)
    rm = shift_z(zm1, -1)
    ryp = shift_y(yp1, 1)
    rym = shift_y(ym1, -1)
    rp = shift_z(add(zp2, rp).astype(BF16), 1)
    rm = shift_z(add(zm2, rm).astype(BF16), -1)
    ryp2 = shift_y(add(a1a, ryp[:4]).astype(BF16), 1)
    rym2 = shift_y(add(a3b, rym[:4]).astype(BF16), -1)
    rp = shift_z(add(zp3, rp).astype(BF16), 1)
    rm = shift_z(add(zm3, rm).astype(BF16), -1)
    rp4 = shift_z(add(zp4, rp[:2]).astype(BF16), 1)
    rm4 = shift_z(add(zm4, rm[:2]).astype(BF16), -1)
    ay = [add(a0[d], ryp2[d], rym[4 + d]) for d in range(4)] + [
        add(a0[4 + d], ryp[4 + d], rym2[d]) for d in range(4)
    ]
    a_sum = ay[0]
    a_in = [shift_z(ay[d].astype(BF16), d) for d in range(1, NZ)]
    bz = [add(b0[d], rp4[d], rm[2 + d]) for d in range(2)] + [
        add(b0[2 + d], rp[2 + d], rm4[d]) for d in range(2)
    ]
    b_in = [shift_y(bz[d].astype(BF16), d) for d in range(1, NY)]
    return add(a_sum, *a_in).astype(BF16), add(bz[0], *b_in).astype(BF16)


def body(
    tokens, gate_blocks, up_blocks, down_blocks,
    gate_index, up_index, down_index, gate_count, up_count, down_count,
):
    core = lax.axis_index("core")
    x, yhi = lax.axis_index("x"), lax.axis_index("yhi")
    z = lax.axis_index("z")
    y = 2 * yhi + lax.axis_index("ylo")

    own = jnp.concatenate([gate_blocks[0], up_blocks[0], down_blocks[0]], axis=0)
    left = shift_x(own, 1)
    right = shift_x(own, -1)
    own_pair = swap_core(own)

    def table(index, count):
        live = jnp.arange(SLOTS, dtype=jnp.int32)[None, :] < count[:, None]
        return jnp.where(live, index, FBS)

    tab = jnp.stack(
        [table(gate_index, gate_count), table(up_index, up_count), table(down_index, down_count)]
    )
    tab = jnp.stack([tab, swap_core(tab)]).reshape(-1)
    rows = [lax.rem(x + off, NX) * 2 + yhi for off in (0, 3, 1, 2)]
    meta = jnp.stack([z, y, *rows]).astype(jnp.int32)

    def block_rows(c):
        part = lax.dynamic_slice_in_dim(tokens, c * HALF, HALF, axis=0)
        return jnp.transpose(part.reshape(HALF, 2, BLK), (1, 0, 2))

    keep = block_rows(core)
    got = swap_core(block_rows(1 - core))
    chip = jnp.where(
        core == 0,
        jnp.concatenate([keep, got], axis=0),
        jnp.concatenate([got, keep], axis=0),
    )
    y0 = jnp.stack([chip, shift_y(chip, -1), shift_y(chip, 2), shift_y(chip, 1)])
    p1, m1 = shift_z(y0, 1), shift_z(y0, -1)
    p2, m2 = shift_z(p1, 1), shift_z(m1, -1)
    p2, m2, tab, meta, own_pair = lax.optimization_barrier((p2, m2, tab, meta, own_pair))
    p3, m3 = shift_z(p2, 1), shift_z(m2, -1)
    left, right, p3, m3 = lax.optimization_barrier((left, right, p3, m3))
    cut = 3 * SLOTS // 2
    far_a = shift_x(left[:cut], 1)
    far_b = shift_x(right[cut:], -1)
    h0, h1 = shift_z(p3[:2], 1), shift_z(m3[2:], -1)

    weights = (own, own_pair, left, swap_core(left), right, swap_core(right))
    acc, x_all = run_first(tab, meta, (y0, p1, p2, p3, m1, m2, m3, h0, h1), weights)
    far_a, far_b, acc = lax.optimization_barrier((far_a, far_b, acc))
    halves = (far_a, far_b, swap_core(far_a), swap_core(far_b))
    parts = run_last(tab, meta, acc, x_all, halves)

    a_fin, b_fin = reduce_scatter(parts)
    mine = jnp.where(core == 0, a_fin, b_fin)
    other = swap_core(jnp.where(core == 0, b_fin, a_fin))
    low = jnp.where(core == 0, mine, other)
    high = jnp.where(core == 0, other, mine)
    out = jnp.stack([low, high])
    return jnp.transpose(out, (0, 2, 1, 3)).reshape(2 * HALF, 2 * BLK)


def solution(mesh):
    fine = Mesh(mesh.devices.reshape(NZ, 2, 2, NX, 2), AXES)
    fsdp, tp = ("z", "ylo", "core"), ("x", "yhi")
    blocks = P(fsdp + tp, None, None, None)
    in_specs = (
        P(tp, fsdp), blocks, blocks, blocks,
        P(fsdp, None), P(fsdp, None), P(fsdp, None), P(fsdp), P(fsdp), P(fsdp),
    )
    return jax.shard_map(
        body, mesh=fine, in_specs=in_specs, out_specs=P(tp, fsdp), check_vma=False
    )
```
